32 devices in a mesh: seq: 4 (over x, core), dp: 8 (over z, y).
Axes of the slice: x: 2, y: 2, z: 4, core: 2. Of those that a mesh axis runs over, the one named last changes fastest.
Arguments:
- attn_mix: bfloat16 [8, 512, 640], P('dp', 'seq'), may hold values from -6 to 6
- resid: bfloat16 [8, 512, 1280], P('dp', 'seq'), may hold values from -6 to 6
- out_weight: bfloat16 [640, 1280], P('dp'), may hold values from -0.25 to 0.25
- merger_norm_gain: float32 [1280], replicated, may hold values from 0.4 to 1.6
- merger_norm_bias: float32 [1280], replicated, may hold values from -1.5 to 1.5
- target: int32 [8, 128], P('dp'), may hold values from 0 to 511, as said below
- token_grad: bfloat16 [8, 512, 5120], P('dp', 'seq'), may hold values from -6 to 6
Outputs:
- token_rows: bfloat16 [8, 512, 5120], P('dp', 'seq')
- resid_grad: bfloat16 [8, 512, 1280], P('dp', 'seq')
- attn_grad: bfloat16 [8, 512, 640], P('dp', 'seq')
The draws below stay inside these ranges and needn't reach their ends.
Inputs may be any that keep to these rules, and one draw needn't show every extreme that they name: `target`: within one packed sequence the entries are distinct. Merged row m is held by seq device m // 32; position p belongs to seq device p // 128. The rows of one seq device name at most 13 positions of any one device, and in every packed sequence some device receives exactly 13 rows from every device.
All inputs are finite; a program needn't handle non-finite values.
Results may differ from the reference program's by a relative error of at most 0.0049.
Values may be sent and summed in bfloat16 or wider, within the bound.
A program may use at most 64 MiB of HBM per device.

```python
import jax
import jax.numpy as jnp
from jax import lax

VW = 1280
VC = 640
MW = 5120
TOK_DEV = 128
MERGED_DEV = 32
CAP = 13
PATCHES = 512
TOKENS = 512
GROUPS = 8
N_SEQ = 4


def draw_target(key, part):

    def one_group(group_key):
        key_hot, key_pick, key_rows, key_slots = jax.random.split(group_key, 4)
        width = N_SEQ * CAP
        hot = jax.random.randint(key_hot, (), 0, N_SEQ)
        cand_owner = jnp.arange(width) // CAP
        noise = jax.random.randint(key_pick, (N_SEQ, width), 0, 1 << 20)
        score = noise * width + jnp.arange(width)[None, :]
        score = jnp.where(cand_owner[None, :] == hot, jnp.arange(width)[None, :] - width, score)
        order = jnp.argsort(score, axis=1)
        chosen = cand_owner[order[:, :MERGED_DEV]]
        row_noise = jax.random.randint(key_rows, (N_SEQ, MERGED_DEV), 0, 1 << 20)
        row_perm = jnp.argsort(row_noise * MERGED_DEV + jnp.arange(MERGED_DEV)[None, :], axis=1)
        owners = jnp.take_along_axis(chosen, row_perm, axis=1)
        flat = owners.reshape(-1)
        hits = (flat[:, None] == jnp.arange(N_SEQ)[None, :]).astype(jnp.int32)
        ranks = jnp.sum((jnp.cumsum(hits, axis=0) - hits) * hits, axis=1)
        slot_noise = jax.random.randint(key_slots, (N_SEQ, TOK_DEV), 0, 1 << 20)
        slot_perm = jnp.argsort(slot_noise * TOK_DEV + jnp.arange(TOK_DEV)[None, :], axis=1)
        slots = slot_perm[flat, ranks]
        return (flat * TOK_DEV + slots).astype(jnp.int32)
    group_keys = jax.vmap(lambda index: jax.random.fold_in(key, index))(jnp.arange(GROUPS))
    return jax.vmap(one_group)(group_keys)


def steps_of(stream_key, shape, cuts, smallest, top_value):
    factor_of = 1.0
    for dim, parts in cuts:
        steps = jax.random.uniform(jax.random.fold_in(jax.random.fold_in(stream_key, 6), dim), (parts,), jnp.float32, smallest / len(cuts), top_value / len(cuts))
        factor_of = factor_of * jnp.repeat(jnp.exp(steps), shape[dim] // parts).reshape((-1,) + (1,) * (len(shape) - 1 - dim))
    return factor_of


def scatter_about(rng, shape, scale, limit, pieces=(), held_as=jnp.bfloat16):
    result = scale * jax.random.normal(rng, shape, jnp.float32)
    if pieces:
        result = result * steps_of(rng, shape, pieces, -0.22, 0.18)
    return jnp.clip(result, -limit, limit).astype(held_as)


def setup_inputs(seed: int = 0) -> dict:
    key_of = jax.random.split(jax.random.key(seed), 8)
    return {
        "attn_mix": scatter_about(key_of[0], (GROUPS, PATCHES, VC), 1.0, 6.0, ((0, 8), (1, 4))),
        "resid": scatter_about(key_of[1], (GROUPS, PATCHES, VW), 1.0, 6.0, ((0, 8), (1, 4))),
        "out_weight": scatter_about(key_of[2], (VC, VW), VC ** -0.5, 0.25, ((0, 8),)),
        "merger_norm_gain": jnp.clip(1.0 + 0.12 * jax.random.normal(key_of[3], (VW,), jnp.float32), 0.4, 1.6),
        "merger_norm_bias": scatter_about(key_of[4], (VW,), 0.3, 1.5, (), jnp.float32),
        "target": draw_target(jax.random.fold_in(key_of[7], 71), 0),
        "token_grad": scatter_about(key_of[6], (GROUPS, TOKENS, MW), 1.0, 6.0, ((0, 8), (1, 4))),
    }


EPS = 1e-06

def reference(attn_mix, resid, out_weight, merger_norm_gain, merger_norm_bias, target, token_grad):

    def one_group(carry, items):
        mix, res, where, tgrad = items
        hidden = res.astype(jnp.float32) + jnp.dot(mix, out_weight, preferred_element_type=jnp.float32)
        row_average = lax.optimization_barrier(jnp.mean(hidden, axis=-1, keepdims=True))
        centered_rows = hidden - row_average
        var = lax.optimization_barrier(jnp.mean(centered_rows * centered_rows, axis=-1, keepdims=True))
        inverse_deviation = lax.rsqrt(var + EPS)
        standardized_input = centered_rows * inverse_deviation
        normalized_rows = (standardized_input * merger_norm_gain + merger_norm_bias).astype(jnp.bfloat16)
        merged = normalized_rows.reshape(-1, MW)
        rows = jnp.zeros((TOKENS, MW), jnp.bfloat16).at[where].set(merged)
        back = tgrad[where].reshape(-1, VW).astype(jnp.float32)
        output_gradient = back * merger_norm_gain
        hidden_gradient = inverse_deviation * (output_gradient - lax.optimization_barrier(jnp.mean(output_gradient, axis=-1, keepdims=True)) - standardized_input * lax.optimization_barrier(jnp.mean(output_gradient * standardized_input, axis=-1, keepdims=True)))
        rgrad = hidden_gradient.astype(jnp.bfloat16)
        agrad = jnp.dot(rgrad, out_weight.T, preferred_element_type=jnp.float32).astype(jnp.bfloat16)
        return (carry, (rows, rgrad, agrad))
    carry, outs = lax.scan(one_group, jnp.zeros((), jnp.float32), (attn_mix, resid, target, token_grad))
    token_rows, resid_grad, attn_grad = outs
    return (token_rows, resid_grad, attn_grad)
```

```python
import functools
import math

import jax
import jax.numpy as jnp
from jax import lax
from jax.experimental import pallas as pl
from jax.experimental.pallas import tpu as pltpu
from jax.sharding import PartitionSpec as P

EPS = 1e-06
F32 = jnp.float32
BF16 = jnp.bfloat16
MESH = pl.DeviceIdType.MESH


def iota(shape, axis):
    return lax.broadcasted_iota(jnp.int32, shape, axis)


def remote(src, dst, send, recv, device):
    return pltpu.make_async_remote_copy(
        src_ref=src, dst_ref=dst, send_sem=send, recv_sem=recv,
        device_id=device, device_id_type=MESH,
    )


def kernel(dims, mix_hbm, resid_hbm, w_hbm, gain_ref, bias_ref, target_ref, tg_hbm,
           rows_hbm, rgrad_hbm, agrad_hbm,
           mix, resid, tg, wbuf, bsend, brecv, fsend, frecv, xhat_s, rows_s, rgrad_s, agrad_s,
           load_sem, own_sem, zsend, ysend, psend, wrecv, precv, bs_sem, br_sem, fs_sem, fr_sem,
           out_sem):
    S, D, A, B, cap, R, wcuts, fcuts = dims
    n_tok, wide = tg.shape
    patches, width = resid.shape
    M = target_ref.shape[1]
    merged = M // S
    group = patches // merged
    half = width // 2
    depth = wbuf.shape[2]
    SR = S * R
    me = lax.axis_index("seq")
    d = lax.axis_index("dp")
    a, b = d // B, d % B
    h = me % 2
    partner = me + 1 - 2 * h

    loads = [
        pltpu.make_async_copy(w_hbm.at[:, i * half:(i + 1) * half], wbuf.at[i, d], own_sem.at[i])
        for i in range(2)
    ]
    tg_load = pltpu.make_async_copy(tg_hbm.at[0], tg, load_sem.at[0])
    mix_load = pltpu.make_async_copy(mix_hbm.at[0], mix, load_sem.at[1])
    resid_load = pltpu.make_async_copy(resid_hbm.at[0], resid, load_sem.at[2])
    for c in loads + [tg_load, mix_load, resid_load]:
        c.start()

    barrier = pltpu.get_barrier_semaphore()
    for r in range(1, S):
        pl.semaphore_signal(barrier, inc=1, device_id={"seq": lax.rem(me + r, S)}, device_id_type=MESH)
    for r in range(1, B):
        pl.semaphore_signal(barrier, inc=1, device_id={"dp": a * B + lax.rem(b + r, B)}, device_id_type=MESH)

    @pl.when(a > 0)
    def _():
        pl.semaphore_signal(barrier, inc=1, device_id={"dp": d - B}, device_id_type=MESH)

    @pl.when(a < A - 1)
    def _():
        pl.semaphore_signal(barrier, inc=1, device_id={"dp": d + B}, device_id_type=MESH)

    for c in loads:
        c.wait()
    ends = jnp.where(a > 0, 1, 0) + jnp.where(a < A - 1, 1, 0)
    pl.semaphore_wait(barrier, S - 1 + B - 1 + ends)

    nc = len(wcuts)

    def piece(half_index, shard, c):
        lo, hi = wcuts[c]
        return wbuf.at[half_index, shard, :, lo:hi]

    def z_copy(src_a, side, k, c):
        p = piece(h, src_a * B + b, c)
        return remote(p, p, zsend.at[0 if side > 0 else 1, k, c],
                      wrecv.at[src_a * B + b, c], {"dp": d - side * B})

    def y_copy(src_a, r, c):
        p = piece(h, src_a * B + b, c)
        return remote(p, p, ysend.at[src_a, r - 1, c], wrecv.at[src_a * B + b, c],
                      {"dp": a * B + lax.rem(b + r, B)})

    def p_copy(shard, c):
        p = piece(h, shard, c)
        return remote(p, p, psend.at[shard, c], precv.at[shard, c], {"seq": partner})

    def arrived(shard, c):
        p = piece(h, shard, c)
        remote(p, p, psend.at[shard, c], wrecv.at[shard, c], {"seq": partner}).wait_recv()

    def each_z(k, side, act):
        src = a + side * k
        ok = jnp.logical_and(src >= 0, src < A)
        onward = jnp.logical_and(a - side >= 0, a - side < A)

        @pl.when(jnp.logical_and(ok, onward))
        def _():
            act(src)

    for c in range(nc):
        for side in (1, -1):
            each_z(0, side, lambda src, side=side, c=c: z_copy(src, side, 0, c).start())
        for r in range(1, B):
            y_copy(a, r, c).start()

    t_row = target_ref[...].astype(F32)
    diag = iota((M, M), 0) == iota((M, M), 1)
    t_col = jnp.sum(jnp.where(diag, jnp.broadcast_to(t_row, (M, M)), 0.0), axis=1, keepdims=True)

    def bucket(v, size):
        out = jnp.zeros(v.shape, F32)
        for o in range(1, S):
            out = out + jnp.where(v >= float(o * size), 1.0, 0.0)
        return out

    own_row, own_col = bucket(t_row, n_tok), bucket(t_col, n_tok)
    place_col = t_col - own_col * n_tok
    m_row, m_col = iota((1, M), 1).astype(F32), iota((M, 1), 0).astype(F32)
    blk_row, blk_col = bucket(m_row, merged), bucket(m_col, merged)
    same = (own_col == own_row) & (blk_col == blk_row) & (m_row < m_col)
    rank_col = jnp.sum(jnp.where(same, 1.0, 0.0), axis=1, keepdims=True)
    me_f = me.astype(F32)

    def relative(v):
        u = v - me_f
        return jnp.where(u < 0.0, u + float(S), u)

    tok_row = iota((1, n_tok), 1).astype(F32)
    hit = (place_col == tok_row) & (own_col == me_f)
    st_row = jnp.sum(jnp.where(hit, relative(blk_col) * R + rank_col + 1.0, 0.0), axis=0, keepdims=True)
    st_row = jnp.where(st_row > 0.0, st_row - 1.0, -4.0 * SR)
    slot_col = iota((SR, 1), 0).astype(F32)
    take = jnp.concatenate(
        [jnp.where(slot_col == st_row + float(j * cap), 1.0, 0.0).astype(BF16) for j in range(group)], axis=1
    )
    tg_load.wait()
    stacked = jnp.concatenate([tg[:, j * width:(j + 1) * width] for j in range(group)], axis=0)
    back_rows = jnp.dot(take, stacked, preferred_element_type=F32)
    back_rows = back_rows.reshape(S, R // 8, 8, width).astype(BF16)
    brecv[0] = back_rows[0]
    bsend[...] = back_rows[1:]

    def b_copy(r):
        return remote(bsend.at[r - 1], brecv.at[S - r], bs_sem.at[r - 1], br_sem.at[S - r - 1],
                      {"seq": lax.rem(me + r, S)})

    for r in range(1, S):
        b_copy(r).start()

    p_int = iota((1, patches), 1)
    p_blk = jnp.zeros((1, patches), F32)
    for o in range(1, merged):
        p_blk = p_blk + jnp.where(p_int >= o * group, 1.0, 0.0)
    p_sub = p_int.astype(F32) - p_blk * group
    mine = m_col == p_blk + me_f * merged
    ps_row = jnp.sum(jnp.where(mine, relative(own_col) * R + rank_col, 0.0), axis=0, keepdims=True)
    ps_row = ps_row + p_sub * cap
    pack = jnp.where(slot_col == ps_row, 1.0, 0.0).astype(BF16)
    p_diag = iota((patches, patches), 0) == iota((patches, patches), 1)
    ps_col = jnp.sum(jnp.where(p_diag, jnp.broadcast_to(ps_row, (patches, patches)), 0.0), axis=1, keepdims=True)
    slot_row = iota((1, SR), 1).astype(F32)
    unpack = jnp.where(ps_col == slot_row, 1.0, 0.0).astype(BF16)
    t_diag = iota((n_tok, n_tok), 0) == iota((n_tok, n_tok), 1)
    st_col = jnp.sum(jnp.where(t_diag, jnp.broadcast_to(st_row, (n_tok, n_tok)), 0.0), axis=1, keepdims=True)
    put = jnp.concatenate(
        [jnp.where(st_col + float(j * cap) == slot_row, 1.0, 0.0).astype(BF16) for j in range(group)], axis=0
    )

    def y_arrivals(k):
        for c in range(nc):
            for side in ((1,) if k == 0 else (1, -1)):
                src = a + side * k

                @pl.when(jnp.logical_and(src >= 0, src < A))
                def _(src=src, c=c):
                    for r in range(1, B):
                        shard = src * B + lax.rem(b + r, B)
                        arrived(shard, c)
                        p_copy(shard, c).start()

    for k in range(1, A):
        for c in range(nc):
            for side in (1, -1):
                src = a + side * k

                @pl.when(jnp.logical_and(src >= 0, src < A))
                def _(src=src, side=side, k=k, c=c):
                    arrived(src * B + b, c)
                    for r in range(1, B):
                        y_copy(src, r, c).start()
                    if k < A - 1:
                        each_z(k, side, lambda s: z_copy(s, side, k, c).start())
                    p_copy(src * B + b, c).start()
        y_arrivals(k - 1)
    y_arrivals(A - 1)

    def other_shards(act):
        @pl.loop(0, D)
        def _(shard):
            @pl.when(shard != d)
            def _():
                for c in range(nc):
                    act(shard, c)

    def p_wait(shard, c):
        p = piece(1 - h, shard, c)
        remote(p, p, psend.at[shard, c], precv.at[shard, c], {"seq": partner}).wait_recv()

    other_shards(p_wait)

    def weight(i):
        if depth % 16 == 0:
            return wbuf[i].reshape(D * depth, half)
        return jnp.concatenate([wbuf[i, s].astype(F32) for s in range(D)], axis=0).astype(BF16)

    mix_load.wait()
    resid_load.wait()
    w = [weight(i) for i in range(2)]
    hidden = resid[...].astype(F32) + jnp.concatenate(
        [jnp.dot(mix[...], w[i], preferred_element_type=F32) for i in range(2)], axis=1
    )
    centered = hidden - jnp.mean(hidden, axis=-1, keepdims=True)
    rstd = lax.rsqrt(jnp.mean(centered * centered, axis=-1, keepdims=True) + EPS)
    xhat = centered * rstd
    xhat_s[...] = xhat
    normed = (xhat * gain_ref[...] + bias_ref[...]).astype(BF16)

    def f_copy(c, r):
        lo, hi = fcuts[c]
        return remote(fsend.at[r - 1, :, :, lo:hi], frecv.at[S - r, :, :, lo:hi],
                      fs_sem.at[c, r - 1], fr_sem.at[c, S - r - 1], {"seq": lax.rem(me + r, S)})

    for c, (lo, hi) in enumerate(fcuts):
        out = jnp.dot(pack, normed[:, lo:hi], preferred_element_type=F32)
        out = out.reshape(S, R // 8, 8, hi - lo).astype(BF16)
        frecv[0, :, :, lo:hi] = out[0]
        fsend[:, :, :, lo:hi] = out[1:]
        for r in range(1, S):
            f_copy(c, r).start()

    for r in range(1, S):
        b_copy(S - r).wait_recv()
    returned = brecv[...].astype(F32).reshape(SR, width).astype(BF16)
    gy = jnp.dot(unpack, returned, preferred_element_type=F32) * gain_ref[...]
    xh = xhat_s[...]
    hg = rstd * (gy - jnp.mean(gy, axis=-1, keepdims=True) - xh * jnp.mean(gy * xh, axis=-1, keepdims=True))
    rgrad = hg.astype(BF16)
    rgrad_s[...] = rgrad
    rg_out = pltpu.make_async_copy(rgrad_s, rgrad_hbm.at[0], out_sem.at[0])
    rg_out.start()
    agrad = sum(
        lax.dot_general(rgrad[:, i * half:(i + 1) * half], w[i], (((1,), (1,)), ((), ())),
                        preferred_element_type=F32)
        for i in range(2)
    )
    agrad_s[...] = agrad.astype(BF16)
    ag_out = pltpu.make_async_copy(agrad_s, agrad_hbm.at[0], out_sem.at[1])
    ag_out.start()

    outs = [rg_out, ag_out]
    for c, (lo, hi) in enumerate(fcuts):
        for r in range(1, S):
            f_copy(c, S - r).wait_recv()
        got = frecv[:, :, :, lo:hi].astype(F32).reshape(SR, hi - lo).astype(BF16)
        placed = jnp.dot(put, got, preferred_element_type=F32).astype(BF16)
        for j in range(group):
            part = (slice(None), slice(j * width + lo, j * width + hi))
            rows_s[part] = placed[j * n_tok:(j + 1) * n_tok]
            copy = pltpu.make_async_copy(rows_s.at[part], rows_hbm.at[(0,) + part],
                                         out_sem.at[2 + c * group + j])
            copy.start()
            outs.append(copy)

    for c in range(nc):
        for side in (1, -1):
            for k in range(A - 1):
                each_z(k, side, lambda src, side=side, k=k, c=c: z_copy(src, side, k, c).wait_send())
        for src in range(A):
            for r in range(1, B):
                y_copy(src, r, c).wait_send()
    other_shards(lambda shard, c: p_copy(shard, c).wait_send())
    for r in range(1, S):
        b_copy(r).wait_send()
        for c in range(len(fcuts)):
            f_copy(c, r).wait_send()
    for copy in outs:
        copy.wait()


def cuts(total, parts):
    lanes = total // 128
    edges = [128 * (lanes * i // parts) for i in range(parts)] + [total]
    return tuple((edges[i], edges[i + 1]) for i in range(parts))


def body(S, D, attn_mix, resid, out_weight, gain, bias, target, token_grad):
    patches, columns = attn_mix.shape[1:]
    width = resid.shape[2]
    n_tok, wide = token_grad.shape[1:]
    merged = target.shape[1] // S
    group = patches // merged
    cap = 5 * merged // (3 * S)
    R = -(-group * cap // 8) * 8
    B = 2 ** int(math.log2(D) // 2)
    A = D // B
    depth = out_weight.shape[0]
    wcuts = cuts(width // 2, 2)
    fcuts = cuts(width, 5)
    nc, nf = len(wcuts), len(fcuts)
    dims = (S, D, A, B, cap, R, wcuts, fcuts)
    hbm = pl.BlockSpec(memory_space=pl.ANY)
    vmem = pl.BlockSpec(memory_space=pltpu.VMEM)
    dma = pltpu.SemaphoreType.DMA
    return pl.pallas_call(
        functools.partial(kernel, dims),
        out_shape=(
            jax.ShapeDtypeStruct(token_grad.shape, BF16),
            jax.ShapeDtypeStruct(resid.shape, BF16),
            jax.ShapeDtypeStruct(attn_mix.shape, BF16),
        ),
        in_specs=[hbm, hbm, hbm, vmem, vmem, vmem, hbm],
        out_specs=(hbm, hbm, hbm),
        scratch_shapes=[
            pltpu.VMEM((patches, columns), BF16),
            pltpu.VMEM((patches, width), BF16),
            pltpu.VMEM((n_tok, wide), BF16),
            pltpu.VMEM((2, D, depth, width // 2), BF16),
            pltpu.VMEM((S - 1, R // 8, 8, width), BF16),
            pltpu.VMEM((S, R // 8, 8, width), BF16),
            pltpu.VMEM((S - 1, R // 8, 8, width), BF16),
            pltpu.VMEM((S, R // 8, 8, width), BF16),
            pltpu.VMEM((patches, width), F32),
            pltpu.VMEM((n_tok, wide), BF16),
            pltpu.VMEM((patches, width), BF16),
            pltpu.VMEM((patches, columns), BF16),
            dma((3,)), dma((2,)), dma((2, A - 1, nc)), dma((A, B - 1, nc)), dma((D, nc)),
            dma((D, nc)), dma((D, nc)), dma((S - 1,)), dma((S - 1,)), dma((nf, S - 1)),
            dma((nf, S - 1)), dma((2 + nf * group,)),
        ],
        compiler_params=pltpu.CompilerParams(
            collective_id=0, has_side_effects=True, vmem_limit_bytes=60 * 1024 * 1024
        ),
    )(attn_mix, resid, out_weight, gain[None], bias[None], target, token_grad)


def solution(mesh):
    placed = (
        P("dp", "seq", None),
        P("dp", "seq", None),
        P("dp", None),
        P(),
        P(),
        P("dp", None),
        P("dp", "seq", None),
    )
    return jax.shard_map(
        functools.partial(body, mesh.shape["seq"], mesh.shape["dp"]),
        mesh=mesh,
        in_specs=placed,
        out_specs=(P("dp", "seq", None), P("dp", "seq", None), P("dp", "seq", None)),
        check_vma=False,
    )
```

```python
import functools
import math

import jax
import jax.numpy as jnp
from jax import lax
from jax.experimental import pallas as pl
from jax.experimental.pallas import tpu as pltpu
from jax.sharding import PartitionSpec as P

EPS = 1e-06
F32 = jnp.float32
BF16 = jnp.bfloat16
MESH = pl.DeviceIdType.MESH


def iota(shape, axis):
    return lax.broadcasted_iota(jnp.int32, shape, axis)


def remote(src, dst, send, recv, device):
    return pltpu.make_async_remote_copy(
        src_ref=src, dst_ref=dst, send_sem=send, recv_sem=recv,
        device_id=device, device_id_type=MESH,
    )


def kernel(dims, mix_hbm, resid_hbm, w_hbm, gain_ref, bias_ref, target_ref, tg_hbm,
           rows_s, rgrad_s, agrad_s,
           mix, resid, tg, wbuf, bsend, brecv, fsend, frecv, xhat_s,
           load_sem, own_sem, zsend, ysend, psend, wrecv, precv, bs_sem, br_sem, fs_sem, fr_sem):
    S, D, A, B, cap, R, wcuts, fcuts = dims
    n_tok, wide = tg.shape
    gain = gain_ref[...].reshape(1, -1)
    bias = bias_ref[...].reshape(1, -1)
    patches, width = resid.shape
    M = target_ref.shape[1]
    merged = M // S
    group = patches // merged
    half = width // 2
    depth = wbuf.shape[2]
    SR = S * R
    me = lax.axis_index("seq")
    d = lax.axis_index("dp")
    a, b = d // B, d % B
    h = me % 2
    partner = me + 1 - 2 * h

    loads = [
        pltpu.make_async_copy(w_hbm.at[:, i * half:(i + 1) * half], wbuf.at[i, d], own_sem.at[i])
        for i in range(2)
    ]
    tg_load = pltpu.make_async_copy(tg_hbm.at[0], tg, load_sem.at[0])
    mix_load = pltpu.make_async_copy(mix_hbm.at[0], mix, load_sem.at[1])
    resid_load = pltpu.make_async_copy(resid_hbm.at[0], resid, load_sem.at[2])
    for c in loads + [tg_load, mix_load, resid_load]:
        c.start()

    barrier = pltpu.get_barrier_semaphore()
    for r in range(1, S):
        pl.semaphore_signal(barrier, inc=1, device_id={"seq": lax.rem(me + r, S)}, device_id_type=MESH)
    for r in range(1, B):
        pl.semaphore_signal(barrier, inc=1, device_id={"dp": a * B + lax.rem(b + r, B)}, device_id_type=MESH)

    @pl.when(a > 0)
    def _():
        pl.semaphore_signal(barrier, inc=1, device_id={"dp": d - B}, device_id_type=MESH)

    @pl.when(a < A - 1)
    def _():
        pl.semaphore_signal(barrier, inc=1, device_id={"dp": d + B}, device_id_type=MESH)

    for c in loads:
        c.wait()
    ends = jnp.where(a > 0, 1, 0) + jnp.where(a < A - 1, 1, 0)
    pl.semaphore_wait(barrier, S - 1 + B - 1 + ends)

    nc = len(wcuts)

    def piece(half_index, shard, c):
        lo, hi = wcuts[c]
        return wbuf.at[half_index, shard, :, lo:hi]

    def z_copy(src_a, side, k, c):
        p = piece(h, src_a * B + b, c)
        return remote(p, p, zsend.at[0 if side > 0 else 1, k, c],
                      wrecv.at[src_a * B + b, c], {"dp": d - side * B})

    def y_copy(src_a, r, c):
        p = piece(h, src_a * B + b, c)
        return remote(p, p, ysend.at[src_a, r - 1, c], wrecv.at[src_a * B + b, c],
                      {"dp": a * B + lax.rem(b + r, B)})

    def p_copy(shard, c):
        p = piece(h, shard, c)
        return remote(p, p, psend.at[shard, c], precv.at[shard, c], {"seq": partner})

    def arrived(shard, c):
        p = piece(h, shard, c)
        remote(p, p, psend.at[shard, c], wrecv.at[shard, c], {"seq": partner}).wait_recv()

    def each_z(k, side, act):
        src = a + side * k
        ok = jnp.logical_and(src >= 0, src < A)
        onward = jnp.logical_and(a - side >= 0, a - side < A)

        @pl.when(jnp.logical_and(ok, onward))
        def _():
            act(src)

    for c in range(nc):
        for side in (1, -1):
            each_z(0, side, lambda src, side=side, c=c: z_copy(src, side, 0, c).start())
        for r in range(1, B):
            y_copy(a, r, c).start()

    t_row = target_ref[...].astype(F32)
    diag = iota((M, M), 0) == iota((M, M), 1)
    t_col = jnp.sum(jnp.where(diag, jnp.broadcast_to(t_row, (M, M)), 0.0), axis=1, keepdims=True)

    def bucket(v, size):
        out = jnp.zeros(v.shape, F32)
        for o in range(1, S):
            out = out + jnp.where(v >= float(o * size), 1.0, 0.0)
        return out

    own_row, own_col = bucket(t_row, n_tok), bucket(t_col, n_tok)
    place_col = t_col - own_col * n_tok
    m_row, m_col = iota((1, M), 1).astype(F32), iota((M, 1), 0).astype(F32)
    blk_row, blk_col = bucket(m_row, merged), bucket(m_col, merged)
    same = (own_col == own_row) & (blk_col == blk_row) & (m_row < m_col)
    rank_col = jnp.sum(jnp.where(same, 1.0, 0.0), axis=1, keepdims=True)
    me_f = me.astype(F32)

    def relative(v):
        u = v - me_f
        return jnp.where(u < 0.0, u + float(S), u)

    tok_row = iota((1, n_tok), 1).astype(F32)
    hit = (place_col == tok_row) & (own_col == me_f)
    st_row = jnp.sum(jnp.where(hit, relative(blk_col) * R + rank_col + 1.0, 0.0), axis=0, keepdims=True)
    st_row = jnp.where(st_row > 0.0, st_row - 1.0, -4.0 * SR)
    slot_col = iota((SR, 1), 0).astype(F32)
    take = jnp.concatenate(
        [jnp.where(slot_col == st_row + float(j * cap), 1.0, 0.0).astype(BF16) for j in range(group)], axis=1
    )
    tg_load.wait()
    stacked = jnp.concatenate([tg[:, j * width:(j + 1) * width] for j in range(group)], axis=0)
    back_rows = jnp.dot(take, stacked, preferred_element_type=F32)
    back_rows = back_rows.reshape(S, R // 8, 8, width).astype(BF16)
    brecv[0] = back_rows[0]
    bsend[...] = back_rows[1:]

    def b_copy(r):
        return remote(bsend.at[r - 1], brecv.at[S - r], bs_sem.at[r - 1], br_sem.at[S - r - 1],
                      {"seq": lax.rem(me + r, S)})

    for r in range(1, S):
        b_copy(r).start()

    p_int = iota((1, patches), 1)
    p_blk = jnp.zeros((1, patches), F32)
    for o in range(1, merged):
        p_blk = p_blk + jnp.where(p_int >= o * group, 1.0, 0.0)
    p_sub = p_int.astype(F32) - p_blk * group
    mine = m_col == p_blk + me_f * merged
    ps_row = jnp.sum(jnp.where(mine, relative(own_col) * R + rank_col, 0.0), axis=0, keepdims=True)
    ps_row = ps_row + p_sub * cap
    pack = jnp.where(slot_col == ps_row, 1.0, 0.0).astype(BF16)
    p_diag = iota((patches, patches), 0) == iota((patches, patches), 1)
    ps_col = jnp.sum(jnp.where(p_diag, jnp.broadcast_to(ps_row, (patches, patches)), 0.0), axis=1, keepdims=True)
    slot_row = iota((1, SR), 1).astype(F32)
    unpack = jnp.where(ps_col == slot_row, 1.0, 0.0).astype(BF16)
    t_diag = iota((n_tok, n_tok), 0) == iota((n_tok, n_tok), 1)
    st_col = jnp.sum(jnp.where(t_diag, jnp.broadcast_to(st_row, (n_tok, n_tok)), 0.0), axis=1, keepdims=True)
    put = jnp.concatenate(
        [jnp.where(st_col + float(j * cap) == slot_row, 1.0, 0.0).astype(BF16) for j in range(group)], axis=0
    )

    def y_arrivals(k):
        for c in range(nc):
            for side in ((1,) if k == 0 else (1, -1)):
                src = a + side * k

                @pl.when(jnp.logical_and(src >= 0, src < A))
                def _(src=src, c=c):
                    for r in range(1, B):
                        shard = src * B + lax.rem(b + r, B)
                        arrived(shard, c)
                        p_copy(shard, c).start()

    for k in range(1, A):
        for c in range(nc):
            for side in (1, -1):
                src = a + side * k

                @pl.when(jnp.logical_and(src >= 0, src < A))
                def _(src=src, side=side, k=k, c=c):
                    arrived(src * B + b, c)
                    for r in range(1, B):
                        y_copy(src, r, c).start()
                    if k < A - 1:
                        each_z(k, side, lambda s: z_copy(s, side, k, c).start())
                    p_copy(src * B + b, c).start()
        y_arrivals(k - 1)
    y_arrivals(A - 1)

    def other_shards(act):
        @pl.loop(0, D)
        def _(shard):
            @pl.when(shard != d)
            def _():
                for c in range(nc):
                    act(shard, c)

    def p_wait(shard, c):
        p = piece(1 - h, shard, c)
        remote(p, p, psend.at[shard, c], precv.at[shard, c], {"seq": partner}).wait_recv()

    other_shards(p_wait)

    def weight(i):
        if depth % 16 == 0:
            return wbuf[i].reshape(D * depth, half)
        return jnp.concatenate([wbuf[i, s].astype(F32) for s in range(D)], axis=0).astype(BF16)

    mix_load.wait()
    resid_load.wait()
    w = [weight(i) for i in range(2)]
    hidden = resid[...].astype(F32) + jnp.concatenate(
        [jnp.dot(mix[...], w[i], preferred_element_type=F32) for i in range(2)], axis=1
    )
    centered = hidden - jnp.mean(hidden, axis=-1, keepdims=True)
    rstd = lax.rsqrt(jnp.mean(centered * centered, axis=-1, keepdims=True) + EPS)
    xhat = centered * rstd
    xhat_s[...] = xhat
    normed = (xhat * gain + bias).astype(BF16)

    def f_copy(c, r):
        lo, hi = fcuts[c]
        return remote(fsend.at[r - 1, :, :, lo:hi], frecv.at[S - r, :, :, lo:hi],
                      fs_sem.at[c, r - 1], fr_sem.at[c, S - r - 1], {"seq": lax.rem(me + r, S)})

    for c, (lo, hi) in enumerate(fcuts):
        out = jnp.dot(pack, normed[:, lo:hi], preferred_element_type=F32)
        out = out.reshape(S, R // 8, 8, hi - lo).astype(BF16)
        frecv[0, :, :, lo:hi] = out[0]
        fsend[:, :, :, lo:hi] = out[1:]
        for r in range(1, S):
            f_copy(c, r).start()

    for r in range(1, S):
        b_copy(S - r).wait_recv()
    returned = brecv[...].astype(F32).reshape(SR, width).astype(BF16)
    gy = jnp.dot(unpack, returned, preferred_element_type=F32) * gain
    xh = xhat_s[...]
    hg = rstd * (gy - jnp.mean(gy, axis=-1, keepdims=True) - xh * jnp.mean(gy * xh, axis=-1, keepdims=True))
    rgrad = hg.astype(BF16)
    rgrad_s[0] = rgrad
    agrad = sum(
        lax.dot_general(rgrad[:, i * half:(i + 1) * half], w[i], (((1,), (1,)), ((), ())),
                        preferred_element_type=F32)
        for i in range(2)
    )
    agrad_s[0] = agrad.astype(BF16)

    for c, (lo, hi) in enumerate(fcuts):
        for r in range(1, S):
            f_copy(c, S - r).wait_recv()
        got = frecv[:, :, :, lo:hi].astype(F32).reshape(SR, hi - lo).astype(BF16)
        placed = jnp.dot(put, got, preferred_element_type=F32).astype(BF16)
        for j in range(group):
            part = (slice(None), slice(j * width + lo, j * width + hi))
            rows_s[(0,) + part] = placed[j * n_tok:(j + 1) * n_tok]

    for c in range(nc):
        for side in (1, -1):
            for k in range(A - 1):
                each_z(k, side, lambda src, side=side, k=k, c=c: z_copy(src, side, k, c).wait_send())
        for src in range(A):
            for r in range(1, B):
                y_copy(src, r, c).wait_send()
    other_shards(lambda shard, c: p_copy(shard, c).wait_send())
    for r in range(1, S):
        b_copy(r).wait_send()
        for c in range(len(fcuts)):
            f_copy(c, r).wait_send()


def write_out(a_ref, b_ref, c_ref, a_hbm, b_hbm, c_hbm, sems):
    pairs = ((a_ref, a_hbm), (b_ref, b_hbm), (c_ref, c_hbm))
    copies = [pltpu.make_async_copy(src, dst, sems.at[i]) for i, (src, dst) in enumerate(pairs)]
    for copy in copies:
        copy.start()
    for copy in copies:
        copy.wait()


def cuts(total, parts):
    lanes = total // 128
    edges = [128 * (lanes * i // parts) for i in range(parts)] + [total]
    return tuple((edges[i], edges[i + 1]) for i in range(parts))


def body(S, D, attn_mix, resid, out_weight, gain, bias, target, token_grad):
    patches, columns = attn_mix.shape[1:]
    width = resid.shape[2]
    n_tok, wide = token_grad.shape[1:]
    merged = target.shape[1] // S
    group = patches // merged
    cap = 5 * merged // (3 * S)
    R = -(-group * cap // 8) * 8
    B = 2 ** int(math.log2(D) // 2)
    A = D // B
    depth = out_weight.shape[0]
    wcuts = cuts(width // 2, 2)
    fcuts = cuts(width, 5)
    nc, nf = len(wcuts), len(fcuts)
    dims = (S, D, A, B, cap, R, wcuts, fcuts)
    hbm = pl.BlockSpec(memory_space=pltpu.HBM)
    vmem = pl.BlockSpec(memory_space=pltpu.VMEM)
    dma = pltpu.SemaphoreType.DMA
    result_bytes = 2 * (token_grad.size + resid.size + attn_mix.size)
    grant = 60 * 1024 * 1024 - result_bytes - 320 * 1024
    outs = pl.pallas_call(
        functools.partial(kernel, dims),
        out_shape=(
            pltpu.VMEM(token_grad.shape, BF16),
            pltpu.VMEM(resid.shape, BF16),
            pltpu.VMEM(attn_mix.shape, BF16),
        ),
        in_specs=[hbm, hbm, hbm, vmem, vmem, vmem, hbm],
        out_specs=(vmem, vmem, vmem),
        scratch_shapes=[
            pltpu.VMEM((patches, columns), BF16),
            pltpu.VMEM((patches, width), BF16),
            pltpu.VMEM((n_tok, wide), BF16),
            pltpu.VMEM((2, D, depth, width // 2), BF16),
            pltpu.VMEM((S - 1, R // 8, 8, width), BF16),
            pltpu.VMEM((S, R // 8, 8, width), BF16),
            pltpu.VMEM((S - 1, R // 8, 8, width), BF16),
            pltpu.VMEM((S, R // 8, 8, width), BF16),
            pltpu.VMEM((patches, width), F32),
            dma((3,)), dma((2,)), dma((2, A - 1, nc)), dma((A, B - 1, nc)), dma((D, nc)),
            dma((D, nc)), dma((D, nc)), dma((S - 1,)), dma((S - 1,)), dma((nf, S - 1)),
            dma((nf, S - 1)),
        ],
        compiler_params=pltpu.CompilerParams(
            collective_id=0, has_side_effects=True, vmem_limit_bytes=grant
        ),
    )(attn_mix, resid, out_weight, gain, bias, target, token_grad)
    return pl.pallas_call(
        write_out,
        out_shape=tuple(jax.ShapeDtypeStruct(o.shape, o.dtype) for o in outs),
        in_specs=[vmem] * 3,
        out_specs=(hbm,) * 3,
        scratch_shapes=[dma((3,))],
        compiler_params=pltpu.CompilerParams(vmem_limit_bytes=8 * 1024 * 1024),
    )(*outs)


def solution(mesh):
    placed = (
        P("dp", "seq", None),
        P("dp", "seq", None),
        P("dp", None),
        P(),
        P(),
        P("dp", None),
        P("dp", "seq", None),
    )
    return jax.shard_map(
        functools.partial(body, mesh.shape["seq"], mesh.shape["dp"]),
        mesh=mesh,
        in_specs=placed,
        out_specs=(P("dp", "seq", None), P("dp", "seq", None), P("dp", "seq", None)),
        check_vma=False,
    )
```

```python
import functools
import math

import jax
import jax.numpy as jnp
from jax import lax
from jax.experimental import pallas as pl
from jax.experimental.pallas import tpu as pltpu
from jax.sharding import PartitionSpec as P

EPS = 1e-06
F32 = jnp.float32
BF16 = jnp.bfloat16
MESH = pl.DeviceIdType.MESH


def iota(shape, axis):
    return lax.broadcasted_iota(jnp.int32, shape, axis)


def remote(src, dst, send, recv, device):
    return pltpu.make_async_remote_copy(
        src_ref=src, dst_ref=dst, send_sem=send, recv_sem=recv,
        device_id=device, device_id_type=MESH,
    )


def kernel(dims, mix_hbm, resid_hbm, w_hbm, gain_hbm, bias_hbm, target_hbm, tg_hbm,
           rows_s, rgrad_s, agrad_s,
           gain_ref, bias_ref, target_ref, mix, resid, tg, wbuf, bsend, brecv, fsend, frecv, xhat_s,
           load_sem, own_sem, zsend, ysend, psend, wrecv, precv, bs_sem, br_sem, fs_sem, fr_sem):
    S, D, A, B, cap, R, wcuts, fcuts = dims
    n_tok, wide = tg.shape
    patches, width = resid.shape
    M = target_ref.shape[1]
    merged = M // S
    group = patches // merged
    half = width // 2
    depth = wbuf.shape[2]
    SR = S * R
    me = lax.axis_index("seq")
    d = lax.axis_index("dp")
    a, b = d // B, d % B
    h = me % 2
    partner = me + 1 - 2 * h

    loads = [
        pltpu.make_async_copy(w_hbm.at[:, i * half:(i + 1) * half], wbuf.at[i, d], own_sem.at[i])
        for i in range(2)
    ]
    tg_load = pltpu.make_async_copy(tg_hbm.at[0], tg, load_sem.at[0])
    mix_load = pltpu.make_async_copy(mix_hbm.at[0], mix, load_sem.at[1])
    resid_load = pltpu.make_async_copy(resid_hbm.at[0], resid, load_sem.at[2])
    small = [
        pltpu.make_async_copy(src, dst, load_sem.at[3 + i])
        for i, (src, dst) in enumerate(((target_hbm, target_ref), (gain_hbm, gain_ref), (bias_hbm, bias_ref)))
    ]
    for c in loads + small[:1] + [tg_load, mix_load, resid_load] + small[1:]:
        c.start()

    barrier = pltpu.get_barrier_semaphore()
    for r in range(1, S):
        pl.semaphore_signal(barrier, inc=1, device_id={"seq": lax.rem(me + r, S)}, device_id_type=MESH)
    for r in range(1, B):
        pl.semaphore_signal(barrier, inc=1, device_id={"dp": a * B + lax.rem(b + r, B)}, device_id_type=MESH)

    @pl.when(a > 0)
    def _():
        pl.semaphore_signal(barrier, inc=1, device_id={"dp": d - B}, device_id_type=MESH)

    @pl.when(a < A - 1)
    def _():
        pl.semaphore_signal(barrier, inc=1, device_id={"dp": d + B}, device_id_type=MESH)

    for c in loads:
        c.wait()
    ends = jnp.where(a > 0, 1, 0) + jnp.where(a < A - 1, 1, 0)
    pl.semaphore_wait(barrier, S - 1 + B - 1 + ends)

    nc = len(wcuts)

    def piece(half_index, shard, c):
        lo, hi = wcuts[c]
        return wbuf.at[half_index, shard, :, lo:hi]

    def z_copy(src_a, side, k, c):
        p = piece(h, src_a * B + b, c)
        return remote(p, p, zsend.at[0 if side > 0 else 1, k, c],
                      wrecv.at[src_a * B + b, c], {"dp": d - side * B})

    def y_copy(src_a, r, c):
        p = piece(h, src_a * B + b, c)
        return remote(p, p, ysend.at[src_a, r - 1, c], wrecv.at[src_a * B + b, c],
                      {"dp": a * B + lax.rem(b + r, B)})

    def p_copy(shard, c):
        p = piece(h, shard, c)
        return remote(p, p, psend.at[0], precv.at[0], {"seq": partner})

    def arrived(shard, c):
        p = piece(h, shard, c)
        remote(p, p, psend.at[0], wrecv.at[shard, c], {"seq": partner}).wait_recv()

    def each_z(k, side, act):
        src = a + side * k
        ok = jnp.logical_and(src >= 0, src < A)
        onward = jnp.logical_and(a - side >= 0, a - side < A)

        @pl.when(jnp.logical_and(ok, onward))
        def _():
            act(src)

    for c in range(nc):
        for side in (1, -1):
            each_z(0, side, lambda src, side=side, c=c: z_copy(src, side, 0, c).start())
        for r in range(1, B):
            y_copy(a, r, c).start()

    small[0].wait()
    t_row = target_ref[...].astype(F32)
    diag = iota((M, M), 0) == iota((M, M), 1)
    t_col = jnp.sum(jnp.where(diag, jnp.broadcast_to(t_row, (M, M)), 0.0), axis=1, keepdims=True)

    def bucket(v, size):
        out = jnp.zeros(v.shape, F32)
        for o in range(1, S):
            out = out + jnp.where(v >= float(o * size), 1.0, 0.0)
        return out

    own_row, own_col = bucket(t_row, n_tok), bucket(t_col, n_tok)
    place_col = t_col - own_col * n_tok
    m_row, m_col = iota((1, M), 1).astype(F32), iota((M, 1), 0).astype(F32)
    blk_row, blk_col = bucket(m_row, merged), bucket(m_col, merged)
    same = (own_col == own_row) & (blk_col == blk_row) & (m_row < m_col)
    rank_col = jnp.sum(jnp.where(same, 1.0, 0.0), axis=1, keepdims=True)
    me_f = me.astype(F32)

    def relative(v):
        u = v - me_f
        return jnp.where(u < 0.0, u + float(S), u)

    tok_row = iota((1, n_tok), 1).astype(F32)
    hit = (place_col == tok_row) & (own_col == me_f)
    st_row = jnp.sum(jnp.where(hit, relative(blk_col) * R + rank_col + 1.0, 0.0), axis=0, keepdims=True)
    st_row = jnp.where(st_row > 0.0, st_row - 1.0, -4.0 * SR)
    slot_col = iota((SR, 1), 0).astype(F32)
    take = jnp.concatenate(
        [jnp.where(slot_col == st_row + float(j * cap), 1.0, 0.0).astype(BF16) for j in range(group)], axis=1
    )
    tg_load.wait()
    stacked = jnp.concatenate([tg[:, j * width:(j + 1) * width] for j in range(group)], axis=0)
    back_rows = jnp.dot(take, stacked, preferred_element_type=F32)
    back_rows = back_rows.reshape(S, R // 8, 8, width).astype(BF16)
    brecv[0] = back_rows[0]
    bsend[...] = back_rows[1:]

    def b_copy(r):
        return remote(bsend.at[r - 1], brecv.at[S - r], bs_sem.at[r - 1], br_sem.at[S - r - 1],
                      {"seq": lax.rem(me + r, S)})

    for r in range(1, S):
        b_copy(r).start()

    p_int = iota((1, patches), 1)
    p_blk = jnp.zeros((1, patches), F32)
    for o in range(1, merged):
        p_blk = p_blk + jnp.where(p_int >= o * group, 1.0, 0.0)
    p_sub = p_int.astype(F32) - p_blk * group
    mine = m_col == p_blk + me_f * merged
    ps_row = jnp.sum(jnp.where(mine, relative(own_col) * R + rank_col, 0.0), axis=0, keepdims=True)
    ps_row = ps_row + p_sub * cap
    pack = jnp.where(slot_col == ps_row, 1.0, 0.0).astype(BF16)
    p_diag = iota((patches, patches), 0) == iota((patches, patches), 1)
    ps_col = jnp.sum(jnp.where(p_diag, jnp.broadcast_to(ps_row, (patches, patches)), 0.0), axis=1, keepdims=True)
    slot_row = iota((1, SR), 1).astype(F32)
    unpack = jnp.where(ps_col == slot_row, 1.0, 0.0).astype(BF16)
    t_diag = iota((n_tok, n_tok), 0) == iota((n_tok, n_tok), 1)
    st_col = jnp.sum(jnp.where(t_diag, jnp.broadcast_to(st_row, (n_tok, n_tok)), 0.0), axis=1, keepdims=True)
    put = jnp.concatenate(
        [jnp.where(st_col + float(j * cap) == slot_row, 1.0, 0.0).astype(BF16) for j in range(group)], axis=0
    )

    def y_arrivals(k):
        for c in range(nc):
            for side in ((1,) if k == 0 else (1, -1)):
                src = a + side * k

                @pl.when(jnp.logical_and(src >= 0, src < A))
                def _(src=src, c=c):
                    for r in range(1, B):
                        shard = src * B + lax.rem(b + r, B)
                        arrived(shard, c)
                        p_copy(shard, c).start()

    for k in range(1, A):
        for c in range(nc):
            for side in (1, -1):
                src = a + side * k

                @pl.when(jnp.logical_and(src >= 0, src < A))
                def _(src=src, side=side, k=k, c=c):
                    arrived(src * B + b, c)
                    for r in range(1, B):
                        y_copy(src, r, c).start()
                    if k < A - 1:
                        each_z(k, side, lambda s: z_copy(s, side, k, c).start())
                    p_copy(src * B + b, c).start()
        y_arrivals(k - 1)
    y_arrivals(A - 1)

    def all_others(half_index):
        p = wbuf.at[half_index, 0:D - 1]
        return remote(p, p, psend.at[0], precv.at[0], {"seq": partner})

    def weight(i):
        if depth % 16 == 0:
            return wbuf[i].reshape(D * depth, half)
        return jnp.concatenate([wbuf[i, s].astype(F32) for s in range(D)], axis=0).astype(BF16)

    mix_load.wait()
    resid_load.wait()
    for c in small[1:]:
        c.wait()
    gain = gain_ref[...].reshape(1, -1)
    bias = bias_ref[...].reshape(1, -1)
    for turn in range(2):
        if turn == 1:
            all_others(1 - h).wait_recv()
        i = h if turn == 0 else 1 - h
        columns = pl.ds(pl.multiple_of(i * half, 128), half)
        xhat_s[:, columns] = resid[:, columns].astype(F32) + jnp.dot(
            mix[...], weight(i), preferred_element_type=F32
        )
    hidden = xhat_s[...]
    w = [weight(i) for i in range(2)]
    centered = hidden - jnp.mean(hidden, axis=-1, keepdims=True)
    rstd = lax.rsqrt(jnp.mean(centered * centered, axis=-1, keepdims=True) + EPS)
    xhat = centered * rstd
    xhat_s[...] = xhat
    normed = (xhat * gain + bias).astype(BF16)

    def f_copy(c, r):
        lo, hi = fcuts[c]
        return remote(fsend.at[r - 1, :, :, lo:hi], frecv.at[S - r, :, :, lo:hi],
                      fs_sem.at[c, r - 1], fr_sem.at[c, S - r - 1], {"seq": lax.rem(me + r, S)})

    for c, (lo, hi) in enumerate(fcuts):
        out = jnp.dot(pack, normed[:, lo:hi], preferred_element_type=F32)
        out = out.reshape(S, R // 8, 8, hi - lo).astype(BF16)
        frecv[0, :, :, lo:hi] = out[0]
        fsend[:, :, :, lo:hi] = out[1:]
        for r in range(1, S):
            f_copy(c, r).start()

    for r in range(1, S):
        b_copy(S - r).wait_recv()
    returned = brecv[...].astype(F32).reshape(SR, width).astype(BF16)
    gy = jnp.dot(unpack, returned, preferred_element_type=F32) * gain
    xh = xhat_s[...]
    hg = rstd * (gy - jnp.mean(gy, axis=-1, keepdims=True) - xh * jnp.mean(gy * xh, axis=-1, keepdims=True))
    rgrad = hg.astype(BF16)
    rgrad_s[0] = rgrad
    agrad = sum(
        lax.dot_general(rgrad[:, i * half:(i + 1) * half], w[i], (((1,), (1,)), ((), ())),
                        preferred_element_type=F32)
        for i in range(2)
    )
    agrad_s[0] = agrad.astype(BF16)

    for c in range(nc):
        for side in (1, -1):
            for k in range(A - 1):
                each_z(k, side, lambda src, side=side, k=k, c=c: z_copy(src, side, k, c).wait_send())
        for src in range(A):
            for r in range(1, B):
                y_copy(src, r, c).wait_send()
    all_others(h).wait_send()
    for r in range(1, S):
        b_copy(r).wait_send()

    for c, (lo, hi) in enumerate(fcuts):
        for r in range(1, S):
            f_copy(c, S - r).wait_recv()
        got = frecv[:, :, :, lo:hi].astype(F32).reshape(SR, hi - lo).astype(BF16)
        placed = jnp.dot(put, got, preferred_element_type=F32).astype(BF16)
        for j in range(group):
            part = (slice(None), slice(j * width + lo, j * width + hi))
            rows_s[(0,) + part] = placed[j * n_tok:(j + 1) * n_tok]

    for r in range(1, S):
        for c in range(len(fcuts)):
            f_copy(c, r).wait_send()


def write_out(a_ref, b_ref, c_ref, a_hbm, b_hbm, c_hbm, sems):
    pairs = ((a_ref, a_hbm), (b_ref, b_hbm), (c_ref, c_hbm))
    copies = [pltpu.make_async_copy(src, dst, sems.at[i]) for i, (src, dst) in enumerate(pairs)]
    for copy in copies:
        copy.start()
    for copy in copies:
        copy.wait()


def cuts(total, parts):
    lanes = total // 128
    edges = [128 * (lanes * i // parts) for i in range(parts)] + [total]
    return tuple((edges[i], edges[i + 1]) for i in range(parts))


def body(S, D, attn_mix, resid, out_weight, gain, bias, target, token_grad):
    patches, columns = attn_mix.shape[1:]
    width = resid.shape[2]
    n_tok, wide = token_grad.shape[1:]
    merged = target.shape[1] // S
    group = patches // merged
    cap = 5 * merged // (3 * S)
    R = -(-group * cap // 8) * 8
    B = 2 ** int(math.log2(D) // 2)
    A = D // B
    depth = out_weight.shape[0]
    wcuts = cuts(width // 2, 2)
    fcuts = cuts(width, 2)
    nc, nf = len(wcuts), len(fcuts)
    dims = (S, D, A, B, cap, R, wcuts, fcuts)
    hbm = pl.BlockSpec(memory_space=pltpu.HBM)
    vmem = pl.BlockSpec(memory_space=pltpu.VMEM)
    dma = pltpu.SemaphoreType.DMA
    result_bytes = 2 * (token_grad.size + resid.size + attn_mix.size)
    grant = 60 * 1024 * 1024 - result_bytes - 64 * 1024
    outs = pl.pallas_call(
        functools.partial(kernel, dims),
        out_shape=(
            pltpu.VMEM(token_grad.shape, BF16),
            pltpu.VMEM(resid.shape, BF16),
            pltpu.VMEM(attn_mix.shape, BF16),
        ),
        in_specs=[hbm] * 7,
        out_specs=(vmem, vmem, vmem),
        scratch_shapes=[
            pltpu.VMEM(gain.shape, F32),
            pltpu.VMEM(bias.shape, F32),
            pltpu.VMEM(target.shape, jnp.int32),
            pltpu.VMEM((patches, columns), BF16),
            pltpu.VMEM((patches, width), BF16),
            pltpu.VMEM((n_tok, wide), BF16),
            pltpu.VMEM((2, D, depth, width // 2), BF16),
            pltpu.VMEM((S - 1, R // 8, 8, width), BF16),
            pltpu.VMEM((S, R // 8, 8, width), BF16),
            pltpu.VMEM((S - 1, R // 8, 8, width), BF16),
            pltpu.VMEM((S, R // 8, 8, width), BF16),
            pltpu.VMEM((patches, width), F32),
            dma((6,)), dma((2,)), dma((2, A - 1, nc)), dma((A, B - 1, nc)), dma((1,)),
            dma((D, nc)), dma((1,)), dma((S - 1,)), dma((S - 1,)), dma((nf, S - 1)),
            dma((nf, S - 1)),
        ],
        compiler_params=pltpu.CompilerParams(
            collective_id=0, has_side_effects=True, vmem_limit_bytes=grant
        ),
    )(attn_mix, resid, out_weight, gain, bias, target, token_grad)
    return pl.pallas_call(
        write_out,
        out_shape=tuple(jax.ShapeDtypeStruct(o.shape, o.dtype) for o in outs),
        in_specs=[vmem] * 3,
        out_specs=(hbm,) * 3,
        scratch_shapes=[dma((3,))],
        compiler_params=pltpu.CompilerParams(vmem_limit_bytes=8 * 1024 * 1024),
    )(*outs)


def solution(mesh):
    placed = (
        P("dp", "seq", None),
        P("dp", "seq", None),
        P("dp", None),
        P(),
        P(),
        P("dp", None),
        P("dp", "seq", None),
    )
    return jax.shard_map(
        functools.partial(body, mesh.shape["seq"], mesh.shape["dp"]),
        mesh=mesh,
        in_specs=placed,
        out_specs=(P("dp", "seq", None), P("dp", "seq", None), P("dp", "seq", None)),
        check_vma=False,
    )
```

```python
import functools
import math

import jax
import jax.numpy as jnp
from jax import lax
from jax.experimental import pallas as pl
from jax.experimental.pallas import tpu as pltpu
from jax.sharding import PartitionSpec as P

EPS = 1e-06
F32 = jnp.float32
BF16 = jnp.bfloat16
MESH = pl.DeviceIdType.MESH


def iota(shape, axis):
    return lax.broadcasted_iota(jnp.int32, shape, axis)


def remote(src, dst, send, recv, device):
    return pltpu.make_async_remote_copy(
        src_ref=src, dst_ref=dst, send_sem=send, recv_sem=recv,
        device_id=device, device_id_type=MESH,
    )


def kernel(dims, mix_hbm, resid_hbm, w_hbm, gain_hbm, bias_hbm, target_hbm, tg_hbm,
           rows_s, rgrad_s, agrad_s,
           gain_ref, bias_ref, target_ref, mix, resid, tg, wbuf, bsend, brecv, fsend, frecv, xhat_s,
           load_sem, own_sem, zsend, ysend, psend, wrecv, precv, bs_sem, br_sem, fs_sem, fr_sem):
    S, D, A, B, cap, R, wcuts, fcuts = dims
    n_tok, wide = tg.shape
    patches, width = resid.shape
    M = target_ref.shape[1]
    merged = M // S
    group = patches // merged
    half = width // 2
    depth = wbuf.shape[2]
    SR = S * R
    me = lax.axis_index("seq")
    d = lax.axis_index("dp")
    a, b = d // B, d % B
    h = me % 2
    partner = me + 1 - 2 * h

    loads = [
        pltpu.make_async_copy(w_hbm.at[:, i * half:(i + 1) * half], wbuf.at[i, d], own_sem.at[i])
        for i in range(2)
    ]
    tg_load = pltpu.make_async_copy(tg_hbm.at[0], tg, load_sem.at[0])
    mix_load = pltpu.make_async_copy(mix_hbm.at[0], mix, load_sem.at[1])
    resid_load = pltpu.make_async_copy(resid_hbm.at[0], resid, load_sem.at[2])
    small = [
        pltpu.make_async_copy(src, dst, load_sem.at[3 + i])
        for i, (src, dst) in enumerate(((target_hbm, target_ref), (gain_hbm, gain_ref), (bias_hbm, bias_ref)))
    ]
    for c in loads + small[:1] + [tg_load, mix_load, resid_load] + small[1:]:
        c.start()

    barrier = pltpu.get_barrier_semaphore()
    for r in range(1, S):
        pl.semaphore_signal(barrier, inc=1, device_id={"seq": lax.rem(me + r, S)}, device_id_type=MESH)
    for r in range(1, B):
        pl.semaphore_signal(barrier, inc=1, device_id={"dp": a * B + lax.rem(b + r, B)}, device_id_type=MESH)

    @pl.when(a > 0)
    def _():
        pl.semaphore_signal(barrier, inc=1, device_id={"dp": d - B}, device_id_type=MESH)

    @pl.when(a < A - 1)
    def _():
        pl.semaphore_signal(barrier, inc=1, device_id={"dp": d + B}, device_id_type=MESH)

    for c in loads:
        c.wait()
    ends = jnp.where(a > 0, 1, 0) + jnp.where(a < A - 1, 1, 0)
    pl.semaphore_wait(barrier, S - 1 + B - 1 + ends)

    nc = len(wcuts)

    def piece(half_index, shard, c):
        lo, hi = wcuts[c]
        return wbuf.at[half_index, shard, :, lo:hi]

    def z_copy(src_a, side, k, c):
        p = piece(h, src_a * B + b, c)
        return remote(p, p, zsend.at[0 if side > 0 else 1, k, c],
                      wrecv.at[src_a * B + b, c], {"dp": d - side * B})

    def y_copy(src_a, r, c):
        p = piece(h, src_a * B + b, c)
        return remote(p, p, ysend.at[src_a, r - 1, c], wrecv.at[src_a * B + b, c],
                      {"dp": a * B + lax.rem(b + r, B)})

    def p_copy(shard, c):
        p = piece(h, shard, c)
        return remote(p, p, psend.at[0], precv.at[0], {"seq": partner})

    def arrived(shard, c):
        p = piece(h, shard, c)
        remote(p, p, psend.at[0], wrecv.at[shard, c], {"seq": partner}).wait_recv()

    def each_z(k, side, act):
        src = a + side * k
        ok = jnp.logical_and(src >= 0, src < A)
        onward = jnp.logical_and(a - side >= 0, a - side < A)

        @pl.when(jnp.logical_and(ok, onward))
        def _():
            act(src)

    for c in range(nc):
        for side in (1, -1):
            each_z(0, side, lambda src, side=side, c=c: z_copy(src, side, 0, c).start())
        for r in range(1, B):
            y_copy(a, r, c).start()

    small[0].wait()
    t_row = target_ref[...].astype(F32)
    diag = iota((M, M), 0) == iota((M, M), 1)
    t_col = jnp.sum(jnp.where(diag, jnp.broadcast_to(t_row, (M, M)), 0.0), axis=1, keepdims=True)

    def bucket(v, size):
        out = jnp.zeros(v.shape, F32)
        for o in range(1, S):
            out = out + jnp.where(v >= float(o * size), 1.0, 0.0)
        return out

    own_row, own_col = bucket(t_row, n_tok), bucket(t_col, n_tok)
    place_col = t_col - own_col * n_tok
    m_row, m_col = iota((1, M), 1).astype(F32), iota((M, 1), 0).astype(F32)
    blk_row, blk_col = bucket(m_row, merged), bucket(m_col, merged)
    same = (own_col == own_row) & (blk_col == blk_row) & (m_row < m_col)
    rank_col = jnp.sum(jnp.where(same, 1.0, 0.0), axis=1, keepdims=True)
    me_f = me.astype(F32)

    def relative(v):
        u = v - me_f
        return jnp.where(u < 0.0, u + float(S), u)

    tok_row = iota((1, n_tok), 1).astype(F32)
    hit = (place_col == tok_row) & (own_col == me_f)
    st_row = jnp.sum(jnp.where(hit, relative(blk_col) * R + rank_col + 1.0, 0.0), axis=0, keepdims=True)
    st_row = jnp.where(st_row > 0.0, st_row - 1.0, -4.0 * SR)
    slot_col = iota((SR, 1), 0).astype(F32)
    take = jnp.concatenate(
        [jnp.where(slot_col == st_row + float(j * cap), 1.0, 0.0).astype(BF16) for j in range(group)], axis=1
    )
    tg_load.wait()
    stacked = jnp.concatenate([tg[:, j * width:(j + 1) * width] for j in range(group)], axis=0)
    back_rows = jnp.dot(take, stacked, preferred_element_type=F32)
    back_rows = back_rows.reshape(S, R // 8, 8, width).astype(BF16)
    brecv[0] = back_rows[0]
    bsend[...] = back_rows[1:]

    def b_copy(r):
        return remote(bsend.at[r - 1], brecv.at[S - r], bs_sem.at[r - 1], br_sem.at[S - r - 1],
                      {"seq": lax.rem(me + r, S)})

    for r in range(1, S):
        b_copy(r).start()

    p_int = iota((1, patches), 1)
    p_blk = jnp.zeros((1, patches), F32)
    for o in range(1, merged):
        p_blk = p_blk + jnp.where(p_int >= o * group, 1.0, 0.0)
    p_sub = p_int.astype(F32) - p_blk * group
    mine = m_col == p_blk + me_f * merged
    ps_row = jnp.sum(jnp.where(mine, relative(own_col) * R + rank_col, 0.0), axis=0, keepdims=True)
    ps_row = ps_row + p_sub * cap
    pack = jnp.where(slot_col == ps_row, 1.0, 0.0).astype(BF16)
    p_diag = iota((patches, patches), 0) == iota((patches, patches), 1)
    ps_col = jnp.sum(jnp.where(p_diag, jnp.broadcast_to(ps_row, (patches, patches)), 0.0), axis=1, keepdims=True)
    slot_row = iota((1, SR), 1).astype(F32)
    unpack = jnp.where(ps_col == slot_row, 1.0, 0.0).astype(BF16)
    t_diag = iota((n_tok, n_tok), 0) == iota((n_tok, n_tok), 1)
    st_col = jnp.sum(jnp.where(t_diag, jnp.broadcast_to(st_row, (n_tok, n_tok)), 0.0), axis=1, keepdims=True)
    put = jnp.concatenate(
        [jnp.where(st_col + float(j * cap) == slot_row, 1.0, 0.0).astype(BF16) for j in range(group)], axis=0
    )

    def y_arrivals(k):
        for c in range(nc):
            for side in ((1,) if k == 0 else (1, -1)):
                src = a + side * k

                @pl.when(jnp.logical_and(src >= 0, src < A))
                def _(src=src, c=c):
                    for r in range(1, B):
                        shard = src * B + lax.rem(b + r, B)
                        arrived(shard, c)
                        p_copy(shard, c).start()

    for k in range(1, A):
        for c in range(nc):
            for side in (1, -1):
                src = a + side * k

                @pl.when(jnp.logical_and(src >= 0, src < A))
                def _(src=src, side=side, k=k, c=c):
                    arrived(src * B + b, c)
                    for r in range(1, B):
                        y_copy(src, r, c).start()
                    if k < A - 1:
                        each_z(k, side, lambda s: z_copy(s, side, k, c).start())
                    p_copy(src * B + b, c).start()
        y_arrivals(k - 1)
    y_arrivals(A - 1)

    def all_others(half_index):
        p = wbuf.at[half_index, 0:D - 1]
        return remote(p, p, psend.at[0], precv.at[0], {"seq": partner})

    def weight(i):
        if depth % 16 == 0:
            return wbuf[i].reshape(D * depth, half)
        return jnp.concatenate([wbuf[i, s].astype(F32) for s in range(D)], axis=0).astype(BF16)

    mix_load.wait()
    resid_load.wait()
    for c in small[1:]:
        c.wait()
    gain = gain_ref[...].reshape(1, -1)
    bias = bias_ref[...].reshape(1, -1)
    for turn in range(2):
        if turn == 1:
            all_others(1 - h).wait_recv()
        i = h if turn == 0 else 1 - h
        columns = pl.ds(pl.multiple_of(i * half, 128), half)
        xhat_s[:, columns] = resid[:, columns].astype(F32) + jnp.dot(
            mix[...], weight(i), preferred_element_type=F32
        )
    hidden = xhat_s[...]
    w = [weight(i) for i in range(2)]
    centered = hidden - jnp.mean(hidden, axis=-1, keepdims=True)
    rstd = lax.rsqrt(jnp.mean(centered * centered, axis=-1, keepdims=True) + EPS)
    xhat = centered * rstd
    xhat_s[...] = xhat
    normed = (xhat * gain + bias).astype(BF16)

    def f_copy(c, r):
        lo, hi = fcuts[c]
        return remote(fsend.at[r - 1, :, :, lo:hi], frecv.at[S - r, :, :, lo:hi],
                      fs_sem.at[c, r - 1], fr_sem.at[c, S - r - 1], {"seq": lax.rem(me + r, S)})

    for c, (lo, hi) in enumerate(fcuts):
        out = jnp.dot(pack, normed[:, lo:hi], preferred_element_type=F32)
        out = out.reshape(S, R // 8, 8, hi - lo).astype(BF16)
        frecv[0, :, :, lo:hi] = out[0]
        fsend[:, :, :, lo:hi] = out[1:]
        for r in range(1, S):
            f_copy(c, r).start()

    for r in range(1, S):
        b_copy(S - r).wait_recv()
    returned = brecv[...].astype(F32).reshape(SR, width).astype(BF16)
    gy = jnp.dot(unpack, returned, preferred_element_type=F32) * gain
    xh = xhat_s[...]
    hg = rstd * (gy - jnp.mean(gy, axis=-1, keepdims=True) - xh * jnp.mean(gy * xh, axis=-1, keepdims=True))
    rgrad = hg.astype(BF16)
    rgrad_s[0] = rgrad
    agrad = sum(
        lax.dot_general(rgrad[:, i * half:(i + 1) * half], w[i], (((1,), (1,)), ((), ())),
                        preferred_element_type=F32)
        for i in range(2)
    )
    agrad_s[0] = agrad.astype(BF16)

    for c in range(nc):
        for side in (1, -1):
            for k in range(A - 1):
                each_z(k, side, lambda src, side=side, k=k, c=c: z_copy(src, side, k, c).wait_send())
        for src in range(A):
            for r in range(1, B):
                y_copy(src, r, c).wait_send()
    all_others(h).wait_send()
    for r in range(1, S):
        b_copy(r).wait_send()

    for c, (lo, hi) in enumerate(fcuts):
        for r in range(1, S):
            f_copy(c, S - r).wait_recv()
        got = frecv[:, :, :, lo:hi].astype(F32).reshape(SR, hi - lo).astype(BF16)
        placed = jnp.dot(put, got, preferred_element_type=F32).astype(BF16)
        for j in range(group):
            part = (slice(None), slice(j * width + lo, j * width + hi))
            rows_s[(0,) + part] = placed[j * n_tok:(j + 1) * n_tok]

    for r in range(1, S):
        for c in range(len(fcuts)):
            f_copy(c, r).wait_send()


def write_out(a_ref, b_ref, c_ref, a_hbm, b_hbm, c_hbm, sems):
    pairs = ((a_ref, a_hbm), (b_ref, b_hbm), (c_ref, c_hbm))
    copies = [pltpu.make_async_copy(src, dst, sems.at[i]) for i, (src, dst) in enumerate(pairs)]
    for copy in copies:
        copy.start()
    for copy in copies:
        copy.wait()


def cuts(total, parts):
    lanes = total // 128
    edges = [128 * (lanes * i // parts) for i in range(parts)] + [total]
    return tuple((edges[i], edges[i + 1]) for i in range(parts))


def body(S, D, attn_mix, resid, out_weight, gain, bias, target, token_grad):
    patches, columns = attn_mix.shape[1:]
    width = resid.shape[2]
    n_tok, wide = token_grad.shape[1:]
    merged = target.shape[1] // S
    group = patches // merged
    cap = 5 * merged // (3 * S)
    R = -(-group * cap // 8) * 8
    B = 2 ** int(math.log2(D) // 2)
    A = D // B
    depth = out_weight.shape[0]
    wcuts = cuts(width // 2, 5)
    fcuts = cuts(width, 2)
    nc, nf = len(wcuts), len(fcuts)
    dims = (S, D, A, B, cap, R, wcuts, fcuts)
    hbm = pl.BlockSpec(memory_space=pltpu.HBM)
    vmem = pl.BlockSpec(memory_space=pltpu.VMEM)
    dma = pltpu.SemaphoreType.DMA
    result_bytes = 2 * (token_grad.size + resid.size + attn_mix.size)
    grant = 60 * 1024 * 1024 - result_bytes - 64 * 1024
    outs = pl.pallas_call(
        functools.partial(kernel, dims),
        out_shape=(
            pltpu.VMEM(token_grad.shape, BF16),
            pltpu.VMEM(resid.shape, BF16),
            pltpu.VMEM(attn_mix.shape, BF16),
        ),
        in_specs=[hbm] * 7,
        out_specs=(vmem, vmem, vmem),
        scratch_shapes=[
            pltpu.VMEM(gain.shape, F32),
            pltpu.VMEM(bias.shape, F32),
            pltpu.VMEM(target.shape, jnp.int32),
            pltpu.VMEM((patches, columns), BF16),
            pltpu.VMEM((patches, width), BF16),
            pltpu.VMEM((n_tok, wide), BF16),
            pltpu.VMEM((2, D, depth, width // 2), BF16),
            pltpu.VMEM((S - 1, R // 8, 8, width), BF16),
            pltpu.VMEM((S, R // 8, 8, width), BF16),
            pltpu.VMEM((S - 1, R // 8, 8, width), BF16),
            pltpu.VMEM((S, R // 8, 8, width), BF16),
            pltpu.VMEM((patches, width), F32),
            dma((6,)), dma((2,)), dma((2, A - 1, nc)), dma((A, B - 1, nc)), dma((1,)),
            dma((D, nc)), dma((1,)), dma((S - 1,)), dma((S - 1,)), dma((nf, S - 1)),
            dma((nf, S - 1)),
        ],
        compiler_params=pltpu.CompilerParams(
            collective_id=0, has_side_effects=True, vmem_limit_bytes=grant
        ),
    )(attn_mix, resid, out_weight, gain, bias, target, token_grad)
    return pl.pallas_call(
        write_out,
        out_shape=tuple(jax.ShapeDtypeStruct(o.shape, o.dtype) for o in outs),
        in_specs=[vmem] * 3,
        out_specs=(hbm,) * 3,
        scratch_shapes=[dma((3,))],
        compiler_params=pltpu.CompilerParams(vmem_limit_bytes=8 * 1024 * 1024),
    )(*outs)


def solution(mesh):
    placed = (
        P("dp", "seq", None),
        P("dp", "seq", None),
        P("dp", None),
        P(),
        P(),
        P("dp", None),
        P("dp", "seq", None),
    )
    return jax.shard_map(
        functools.partial(body, mesh.shape["seq"], mesh.shape["dp"]),
        mesh=mesh,
        in_specs=placed,
        out_specs=(P("dp", "seq", None), P("dp", "seq", None), P("dp", "seq", None)),
        check_vma=False,
    )
```
